256 devices in a mesh: pb: 64 (over y, z, core), sa: 4 (over x).
Axes of the slice: x: 4, y: 4, z: 8, core: 2. Of those that a mesh axis runs over, the one named last changes fastest.
Arguments:
- queries: bfloat16 [768, 131072], P('sa', 'pb'), may hold values from -6 to 6
- anchor_keys: bfloat16 [1024, 768], P('pb', 'sa'), may hold values from -6 to 6
- anchor_values: bfloat16 [1024, 768], P('pb', 'sa'), may hold values from -6 to 6
- out_grad: bfloat16 [768, 131072], P('sa', 'pb'), may hold values from -48 to 48
- link_cell: int32 [64, 64, 32], P('pb'), may hold values from 0 to 2047
- link_super: int32 [64, 64, 32], P('pb'), may hold values from 0 to 31
- link_count: int32 [64, 64], P('pb'), may hold values from 0 to 32, as said below
Outputs:
- query_grad: bfloat16 [768, 131072], P('sa', 'pb')
- key_grad: float32 [1024, 768], P('pb', 'sa')
- value_grad: float32 [1024, 768], P('pb', 'sa')
- super_grad: float32 [2048, 768], P('pb', 'sa')
The draws below stay inside these ranges and needn't reach their ends.
Inputs may be any that keep to these rules, and one draw needn't show every extreme that they name: Slot [p, o, c] names cell p * 2048 + link_cell[p, o, c]. Slot [p, o, c] names supernode o * 32 + link_super[p, o, c]. Slot c of the list from block p to owner o is valid when c < link_count[p, o]; the other slots are padding and their indices mean nothing. Some owner gets 32 valid slots from every block.
All inputs are finite; a program needn't handle non-finite values.
Results may differ from the reference program's by a relative error of at most 0.012.
Values may be sent and summed in bfloat16 or wider, within the bound.
No kernel may reach another device: no remote copies, remote signals or barrier semaphores. Data moves between devices by JAX's collectives and lax.ppermute only.
A program may use at most 64 MiB of HBM per device.

```python
import math
import jax
import jax.numpy as jnp
from jax import lax

HEADS = 12
HEAD_DIM = 64
D = 768
CELL_DEV = 2048
ANC_DEV = 16
SUP_DEV = 32
CAP = 32
NQ = 131072
NA = 1024
N_PB = 64


def draw_queries(key, part):
    entries = jax.random.normal(jax.random.fold_in(key, 1), (NQ, D), jnp.float32)
    return jnp.transpose(jnp.clip(entries, -6.0, 6.0)).astype(jnp.bfloat16)


def draw_anchor_keys(key, part):
    entries = jax.random.normal(jax.random.fold_in(key, 5), (NA, D), jnp.float32)
    return jnp.clip(entries, -6.0, 6.0).astype(jnp.bfloat16)


def draw_link_count(key, part):
    owner_total = NA // ANC_DEV
    base = jax.random.randint(jax.random.fold_in(key, 21), (owner_total, owner_total), 0, 2 * CAP // 3 + 1)
    hottest = jax.random.randint(jax.random.fold_in(key, 22), (), 0, owner_total)
    owners = jnp.arange(owner_total)[None, :]
    return jnp.where(owners == hottest, CAP, base).astype(jnp.int32)


def with_ends(values, stream_key, smallest, top_value):
    extent = values.shape
    place = [jax.random.randint(jax.random.fold_in(stream_key, axis), (), 0, extent[axis]) for axis in range(len(extent))]
    values = values.at[tuple(place)].set(smallest)
    longest = extent.index(max(extent))
    place[longest] = (place[longest] + 1) % extent[longest]
    return values.at[tuple(place)].set(top_value)


def block_scale(rng, extent, cuts, least, largest):
    def one(position, parts):
        draws = jax.random.uniform(jax.random.fold_in(jax.random.fold_in(rng, 6), position), (parts,), jnp.float32, least / len(cuts), largest / len(cuts))
        return jnp.repeat(jnp.exp(draws), extent[position] // parts).reshape((-1,) + (1,) * (len(extent) - position - 1))

    level = one(*cuts[0])
    for cut in cuts[1:]:
        level = level * one(*cut)
    return level


def gaussian(rng, shape, deviation, reach, cuts=(), kind=jnp.bfloat16):
    values = deviation * jax.random.normal(rng, shape, jnp.float32)
    if cuts:
        values = values * block_scale(rng, shape, cuts, -0.22, 0.18)
    return jnp.clip(values, -reach, reach).astype(kind)


def setup_inputs(seed: int = 0) -> dict:
    key_of = jax.random.split(jax.random.key(seed), 8)
    queries = draw_queries(jax.random.fold_in(key_of[7], 71), 0)
    anchor_keys = draw_anchor_keys(jax.random.fold_in(key_of[7], 71), 0)
    anchor_values = gaussian(key_of[2], (NA, D), 1.0, 6.0, ((0, 64), (1, 4)))
    out_grad = gaussian(key_of[3], (D, NQ), 8.0, 48.0, ((0, 4), (1, 64)))
    link_cell = with_ends(jax.random.randint(key_of[4], (N_PB, N_PB, CAP), 0, CELL_DEV), jax.random.fold_in(key_of[4], 1), 0, CELL_DEV - 1).astype(jnp.int32)
    link_super = with_ends(jax.random.randint(key_of[5], (N_PB, N_PB, CAP), 0, SUP_DEV), jax.random.fold_in(key_of[5], 1), 0, SUP_DEV - 1).astype(jnp.int32)
    link_count = draw_link_count(jax.random.fold_in(key_of[7], 71), 0)
    return {"queries": queries, "anchor_keys": anchor_keys, "anchor_values": anchor_values, "out_grad": out_grad, "link_cell": link_cell, "link_super": link_super, "link_count": link_count}


def reference(queries, anchor_keys, anchor_values, out_grad, link_cell, link_super, link_count):
    score_scale = HEAD_DIM ** -0.5
    query_rows_all = jnp.transpose(queries)
    grad_rows_all = jnp.transpose(out_grad)
    query_count = query_rows_all.shape[0]
    anchor_count = anchor_keys.shape[0]
    block_rows = math.gcd(query_count, 2048)
    block_total = query_count // block_rows
    key_heads = anchor_keys.astype(jnp.float32).reshape(anchor_count, HEADS, HEAD_DIM)
    value_heads = anchor_values.astype(jnp.float32).reshape(anchor_count, HEADS, HEAD_DIM)
    query_blocks = query_rows_all.reshape(block_total, block_rows, HEADS, HEAD_DIM)
    grad_blocks = grad_rows_all.reshape(block_total, block_rows, HEADS, HEAD_DIM)

    def block_step(running, inputs):
        key_acc, value_acc = running
        query_rows = inputs[0].astype(jnp.float32)
        grad_rows = inputs[1].astype(jnp.float32)
        scores = score_scale * jnp.einsum("ihd,ahd->hia", query_rows, key_heads)
        row_max = jnp.max(scores, axis=2, keepdims=True)
        raised = jnp.exp(scores - row_max)
        attend = raised / jnp.sum(raised, axis=2, keepdims=True)
        attend_low = lax.optimization_barrier(attend.astype(jnp.bfloat16)).astype(jnp.float32)
        output = jnp.einsum("hia,ahd->hid", attend_low, value_heads)
        grad_heads = jnp.transpose(grad_rows, (1, 0, 2))
        row_delta = jnp.sum(grad_heads * output, axis=2, keepdims=True)
        grad_attend = jnp.einsum("hid,ahd->hia", grad_heads, value_heads)
        grad_scores = lax.optimization_barrier(
            (score_scale * attend * (grad_attend - row_delta)).astype(jnp.bfloat16)).astype(jnp.float32)
        query_part = jnp.einsum("hia,ahd->ihd", grad_scores, key_heads).astype(jnp.bfloat16)
        key_acc = key_acc + jnp.einsum("hia,ihd->ahd", grad_scores, query_rows)
        value_acc = value_acc + jnp.einsum("hia,hid->ahd", attend_low, grad_heads)
        return (key_acc, value_acc), query_part.reshape(block_rows, HEADS * HEAD_DIM)

    empty = jnp.zeros((anchor_count, HEADS, HEAD_DIM), jnp.float32)
    (key_acc, value_acc), query_parts = lax.scan(block_step, (empty, empty), (query_blocks, grad_blocks))
    query_grad_rows = query_parts.reshape(query_count, HEADS * HEAD_DIM)
    key_grad = key_acc.reshape(anchor_count, HEADS * HEAD_DIM)
    value_grad = value_acc.reshape(anchor_count, HEADS * HEAD_DIM)

    owner_count = link_count.shape[0]
    slots = jnp.arange(CAP, dtype=jnp.int32)
    live_slots = slots[None, None, :] < link_count[:, :, None]
    block_index = jnp.arange(owner_count, dtype=jnp.int32)
    cell_index = (block_index[:, None, None] * CELL_DEV + link_cell).astype(jnp.int32).reshape(-1)
    super_index = jnp.where(live_slots, block_index[None, :, None] * SUP_DEV + link_super,
                            owner_count * SUP_DEV).astype(jnp.int32).reshape(-1)
    picked = query_grad_rows[cell_index].astype(jnp.float32)
    super_grad = jax.ops.segment_sum(picked, super_index, num_segments=owner_count * SUP_DEV + 1)[:owner_count * SUP_DEV]
    return jnp.transpose(query_grad_rows), key_grad, value_grad, super_grad
```

```python
import functools
import math

import jax
import jax.numpy as jnp
from jax import lax
from jax.experimental import pallas as pl
from jax.experimental.pallas import tpu as pltpu
from jax.sharding import PartitionSpec as P

HEAD_DIM = 64
SUP_DEV = 32
N_Y, N_Z, N_CORE = 4, 8, 2
N_PB = N_Y * N_Z * N_CORE
CELL_TILE = 512
ANCHOR_CHUNK = 256
F32 = jnp.float32
BF16 = jnp.bfloat16


def pb_groups(axis):
    ranks = [
        [[(y * N_Z + z) * N_CORE + c for c in range(N_CORE)] for z in range(N_Z)]
        for y in range(N_Y)
    ]
    if axis == "y":
        return [[ranks[y][z][c] for y in range(N_Y)] for z in range(N_Z) for c in range(N_CORE)]
    return [[ranks[y][z][c] for z in range(N_Z)] for y in range(N_Y) for c in range(N_CORE)]


def dot(left, right, left_dim, right_dim):
    return lax.dot_general(
        left, right, (((left_dim,), (right_dim,)), ((), ())), preferred_element_type=F32
    )


def fold(values, op):
    rows, cols = values.shape
    return op(values.reshape(rows // 8, 8, cols), axis=0)


def attention_kernel(
    core_ref, link_ref, q_ref, g_ref, kv_ref, qg_ref, pay_ref,
    kp_ref, vh_ref, kt_ref, s_ref, ga_ref, p_ref, ds_ref, kacc_ref, vacc_ref,
):
    step = pl.program_id(0)
    cols, tile = q_ref.shape
    heads = cols // HEAD_DIM
    anchors = kv_ref.shape[0]
    chunk = ANCHOR_CHUNK
    score_scale = HEAD_DIM ** -0.5

    @pl.when(step == 0)
    def _():
        for h in range(heads):
            keys = kv_ref[:, h * HEAD_DIM : (h + 1) * HEAD_DIM].astype(F32)
            scaled = keys * (score_scale * math.log2(math.e))
            high = scaled.astype(BF16)
            low = (scaled - high.astype(F32)).astype(BF16)
            kp_ref[h] = jnp.concatenate([high, low], axis=1)
            vh_ref[h] = kv_ref[:, cols + h * HEAD_DIM : cols + (h + 1) * HEAD_DIM]
            kt_ref[h] = jnp.transpose(keys * score_scale).astype(BF16)
        kacc_ref[...] = jnp.zeros_like(kacc_ref)
        vacc_ref[...] = jnp.zeros_like(vacc_ref)

    for h in range(heads):
        rows = slice(h * HEAD_DIM, (h + 1) * HEAD_DIM)
        q = q_ref[rows, :]
        g = g_ref[rows, :]
        qq = jnp.concatenate([q, q], axis=0)
        top = None
        for a in range(0, anchors, chunk):
            part = dot(kp_ref[h, a : a + chunk, :], qq, 1, 0)
            s_ref[a : a + chunk, :] = part
            part = fold(part, jnp.max)
            top = part if top is None else jnp.maximum(top, part)
        top = jnp.max(top, axis=0, keepdims=True)
        total = jnp.zeros((8, tile), F32)
        delta = jnp.zeros((8, tile), F32)
        for a in range(0, anchors, chunk):
            p = jnp.exp2(s_ref[a : a + chunk, :] - top)
            ga = dot(vh_ref[h, a : a + chunk, :], g, 1, 0)
            total += fold(p, jnp.sum)
            delta += fold(p * ga, jnp.sum)
            p_ref[a : a + chunk, :] = p.astype(BF16)
            ga_ref[a : a + chunk, :] = ga
        inverse = 1.0 / jnp.sum(total, axis=0, keepdims=True)
        delta = jnp.sum(delta, axis=0, keepdims=True) * inverse
        qr = (q.astype(F32) * inverse).astype(BF16)
        gr = (g.astype(F32) * inverse).astype(BF16)
        for a in range(0, anchors, chunk):
            p = p_ref[a : a + chunk, :]
            ds = p * (ga_ref[a : a + chunk, :] - delta).astype(BF16)
            ds_ref[a : a + chunk, :] = ds
            vacc_ref[h, a : a + chunk, :] += dot(p, gr, 1, 1)
            kacc_ref[h, a : a + chunk, :] += dot(ds, qr, 1, 1)
        qg = dot(kt_ref[h], ds_ref[...], 1, 0) * inverse
        qg_ref[rows, pl.ds(pl.multiple_of(step * tile, tile), tile)] = qg.astype(BF16)

    @pl.when(step == pl.num_programs(0) - 1)
    def _():
        core = core_ref[0]
        per = anchors // N_PB
        half = N_PB // N_CORE
        for h in range(heads):
            both = jnp.concatenate([kacc_ref[h] * score_scale, vacc_ref[h]], axis=1).astype(BF16)
            for owner in range(N_PB):
                slot = ((owner % N_CORE) ^ core) * half + owner // N_CORE
                pay_ref[slot, 0:per, h * 128 : (h + 1) * 128] = both[owner * per : (owner + 1) * per, :]
        group = link_ref.shape[2] // 32
        cell_iota = lax.broadcasted_iota(jnp.int32, (qg_ref.shape[1], link_ref.shape[2]), 0)
        sup_iota = lax.broadcasted_iota(jnp.int32, (group * 16, link_ref.shape[2]), 0)
        for block in range(link_ref.shape[0]):
            onehot = (cell_iota == link_ref[block, 0:1, :]).astype(F32).astype(BF16)
            picked = dot(qg_ref[...], onehot, 1, 0).astype(BF16)
            low = (sup_iota == link_ref[block, 1:2, :]).astype(F32).astype(BF16)
            high = (sup_iota == link_ref[block, 2:3, :]).astype(F32).astype(BF16)
            sums = jnp.concatenate([dot(low, picked, 1, 1), dot(high, picked, 1, 1)], axis=1).astype(BF16)
            for j in range(group):
                owner = block * group + j
                slot = ((owner % N_CORE) ^ core) * half + owner // N_CORE
                pay_ref[slot, 16:32, :] = sums[j * 16 : (j + 1) * 16, :]


def attention(core, links, queries, out_grad, kv):
    cols, cells = queries.shape
    anchors = kv.shape[0]
    heads = cols // HEAD_DIM
    tile = CELL_TILE
    tile_spec = pl.BlockSpec((cols, tile), lambda i: (0, i))
    whole = lambda shape: pl.BlockSpec(shape, lambda i: (0,) * len(shape))
    payload = (N_PB, 32, 2 * cols)
    return pl.pallas_call(
        attention_kernel,
        grid=(cells // tile,),
        in_specs=[
            pl.BlockSpec(memory_space=pltpu.SMEM),
            whole(links.shape),
            tile_spec,
            tile_spec,
            whole(kv.shape),
        ],
        out_specs=[whole((cols, cells)), whole(payload)],
        out_shape=[
            jax.ShapeDtypeStruct((cols, cells), BF16),
            jax.ShapeDtypeStruct(payload, BF16),
        ],
        scratch_shapes=[
            pltpu.VMEM((heads, anchors, 2 * HEAD_DIM), BF16),
            pltpu.VMEM((heads, anchors, HEAD_DIM), BF16),
            pltpu.VMEM((heads, HEAD_DIM, anchors), BF16),
            pltpu.VMEM((anchors, tile), F32),
            pltpu.VMEM((anchors, tile), F32),
            pltpu.VMEM((anchors, tile), BF16),
            pltpu.VMEM((anchors, tile), BF16),
            pltpu.VMEM((heads, anchors, HEAD_DIM), F32),
            pltpu.VMEM((heads, anchors, HEAD_DIM), F32),
        ],
        compiler_params=pltpu.CompilerParams(
            dimension_semantics=("arbitrary",), vmem_limit_bytes=60 << 20
        ),
        name="attention_grad",
    )(core, links, queries, out_grad, kv)


def link_table(link_cell, link_super, link_count):
    owners, slots = link_cell.shape
    group = 8
    live = jnp.arange(slots, dtype=jnp.int32)[None, :] < link_count[:, None]
    place = (jnp.arange(owners, dtype=jnp.int32) % group)[:, None] * 16
    cell = jnp.where(live, link_cell, -1)
    low = jnp.where(live & (link_super < 16), place + link_super, -1)
    high = jnp.where(live & (link_super >= 16), place + link_super - 16, -1)
    table = jnp.stack([cell, low, high], axis=0).reshape(3, owners // group, group * slots)
    return jnp.transpose(table, (1, 0, 2))


def local(queries, anchor_keys, anchor_values, out_grad, link_cell, link_super, link_count):
    cols = queries.shape[0]
    heads = cols // HEAD_DIM
    pair = jnp.concatenate([anchor_keys, anchor_values], axis=1)
    copies = jnp.broadcast_to(pair[None], (N_PB,) + pair.shape)
    kv = lax.all_to_all(copies, "pb", 0, 0, tiled=True).reshape(-1, 2 * cols)
    links = link_table(link_cell[0], link_super[0], link_count[0])
    core = (lax.axis_index("pb") % N_CORE).astype(jnp.int32).reshape(1)
    query_grad, pay = attention(core, links, queries, out_grad, kv)

    half = N_PB // N_CORE
    partner = [(i, i ^ 1) for i in range(N_PB)]
    other = lax.ppermute(pay[half:], "pb", partner)
    part = (pay[:half].astype(F32) + other.astype(F32)).astype(BF16)
    part = part.reshape(N_Y, N_Z, 32, 2 * cols)
    part = lax.all_to_all(part, "pb", 0, 0, axis_index_groups=pb_groups("y"), tiled=True)
    part = jnp.sum(part.astype(F32), axis=0).astype(BF16)
    part = lax.all_to_all(part, "pb", 0, 0, axis_index_groups=pb_groups("z"), tiled=True)
    part = jnp.sum(part.astype(F32), axis=0)
    anchor_part = part[:16].reshape(16, heads, 2, HEAD_DIM)
    key_grad = anchor_part[:, :, 0].reshape(16, cols)
    value_grad = anchor_part[:, :, 1].reshape(16, cols)
    super_part = part[16:].reshape(16, 2, cols)
    super_grad = jnp.concatenate([super_part[:, 0], super_part[:, 1]], axis=0)
    return (query_grad, key_grad, value_grad, super_grad)


def solution(mesh):
    return jax.shard_map(
        local,
        mesh=mesh,
        in_specs=(
            P("sa", "pb"),
            P("pb", "sa"),
            P("pb", "sa"),
            P("sa", "pb"),
            P("pb", None, None),
            P("pb", None, None),
            P("pb", None),
        ),
        out_specs=(P("sa", "pb"), P("pb", "sa"), P("pb", "sa"), P("pb", "sa")),
        check_vma=False,
    )
```

```python
import math

import jax
import jax.numpy as jnp
from jax import lax
from jax.experimental import pallas as pl
from jax.experimental.pallas import tpu as pltpu
from jax.sharding import PartitionSpec as P

HEAD_DIM = 64
SUP_DEV = 32
N_Y, N_Z, N_CORE = 4, 8, 2
N_YZ = N_Y * N_Z
N_PB = N_YZ * N_CORE
TILE = 256
CHUNK = 256
GROUP = 8
SPLIT = 256
F32 = jnp.float32
BF16 = jnp.bfloat16


def pb_groups(axis):
    ranks = [
        [[(y * N_Z + z) * N_CORE + c for c in range(N_CORE)] for z in range(N_Z)]
        for y in range(N_Y)
    ]
    if axis == "y":
        return [[ranks[y][z][c] for y in range(N_Y)] for z in range(N_Z) for c in range(N_CORE)]
    if axis == "z":
        return [[ranks[y][z][c] for z in range(N_Z)] for y in range(N_Y) for c in range(N_CORE)]
    return [[ranks[y][z][c] for y in range(N_Y) for z in range(N_Z)] for c in range(N_CORE)]


def dot(left, right, left_dim, right_dim):
    return lax.dot_general(
        left, right, (((left_dim,), (right_dim,)), ((), ())), preferred_element_type=F32
    )


def fold(values, op):
    rows, cols = values.shape
    return op(values.reshape(rows // 8, 8, cols), axis=0)


def attention_kernel(
    link_ref, q_ref, g_ref, mine_ref, other_ref, qg_ref, keep_ref, send_ref,
    kp_ref, vh_ref, kt_ref, s0_ref, s1_ref, ga0_ref, ga1_ref, p0_ref, p1_ref, kacc_ref, vacc_ref,
):
    cols, cells = q_ref.shape
    heads = cols // HEAD_DIM
    half = mine_ref.shape[0]
    anchors = 2 * half
    tiles = cells // TILE
    units = heads * tiles
    score_scale = HEAD_DIM ** -0.5
    chunks = range(0, anchors, CHUNK)
    bufs = ((s0_ref, ga0_ref, p0_ref), (s1_ref, ga1_ref, p1_ref))

    for part, source in enumerate((mine_ref, other_ref)):
        span = slice(part * half, (part + 1) * half)
        for h in range(heads):
            keys = source[:, h * HEAD_DIM : (h + 1) * HEAD_DIM].astype(F32)
            scaled = keys * (score_scale * math.log2(math.e))
            high = scaled.astype(BF16)
            low = (scaled - high.astype(F32)).astype(BF16)
            kp_ref[h, span, :] = jnp.concatenate([high, low], axis=1)
            vh_ref[h, span, :] = source[:, cols + h * HEAD_DIM : cols + (h + 1) * HEAD_DIM]
            kt_ref[h, :, span] = jnp.transpose(keys * score_scale).astype(BF16)
    kacc_ref[...] = jnp.zeros_like(kacc_ref)
    vacc_ref[...] = jnp.zeros_like(vacc_ref)

    def place(unit):
        head = unit // tiles
        rows = pl.ds(pl.multiple_of(head * HEAD_DIM, HEAD_DIM), HEAD_DIM)
        lanes = pl.ds(pl.multiple_of((unit % tiles) * TILE, TILE), TILE)
        return head, rows, lanes

    def step(unit, slot, top, inverse, delta, first=True, second=True, third=True):
        s_next, _, _ = bufs[slot]
        s_now, ga_now, p_now = bufs[1 - slot]
        _, ga_old, p_old = bufs[slot]
        new_top = new_inverse = new_delta = None
        if first:
            head1, rows1, lanes1 = place(unit)
            q1 = q_ref[rows1, lanes1]
            q1 = jnp.concatenate([q1, q1], axis=0)
        if second:
            head2, rows2, lanes2 = place(unit - 1)
            g2 = g_ref[rows2, lanes2]
            total = jnp.zeros((8, TILE), F32)
            moment = jnp.zeros((8, TILE), F32)
        if third:
            head3, rows3, lanes3 = place(unit - 2)
            q3 = (q_ref[rows3, lanes3].astype(F32) * inverse).astype(BF16)
            g3 = (g_ref[rows3, lanes3].astype(F32) * inverse).astype(BF16)
            qg = jnp.zeros((HEAD_DIM, TILE), F32)
        for a in chunks:
            span = slice(a, a + CHUNK)
            if first:
                part = dot(kp_ref[head1, span, :], q1, 1, 0)
                s_next[span, :] = part
                part = fold(part, jnp.max)
                new_top = part if new_top is None else jnp.maximum(new_top, part)
            if third:
                p = p_old[span, :]
                ds = p * (ga_old[span, :] - delta).astype(BF16)
                vacc_ref[head3, :, span] += dot(g3, p, 1, 1)
                kacc_ref[head3, :, span] += dot(q3, ds, 1, 1)
                qg += dot(kt_ref[head3, :, span], ds, 1, 0)
            if second:
                ga = dot(vh_ref[head2, span, :], g2, 1, 0)
                p = jnp.exp2(s_now[span, :] - top)
                total += fold(p, jnp.sum)
                moment += fold(p * ga, jnp.sum)
                p_now[span, :] = p.astype(BF16)
                ga_now[span, :] = ga
        if first:
            new_top = jnp.max(new_top, axis=0, keepdims=True)
        if second:
            new_inverse = 1.0 / jnp.sum(total, axis=0, keepdims=True)
            new_delta = jnp.sum(moment, axis=0, keepdims=True) * new_inverse
        if third:
            qg_ref[rows3, lanes3] = (qg * inverse).astype(BF16)
        return new_top, new_inverse, new_delta

    top, _, _ = step(0, 0, None, None, None, second=False, third=False)
    top, inverse, delta = step(1, 1, top, None, None, third=False)

    def double(i, carry):
        unit = 2 + 2 * i
        carry = step(unit, 0, *carry)
        return step(unit + 1, 1, *carry)

    top, inverse, delta = lax.fori_loop(0, (units - 2) // 2, double, (top, inverse, delta))
    _, inverse, delta = step(units, 0, top, inverse, delta, first=False)
    step(units + 1, 1, None, inverse, delta, first=False, second=False)

    per = half // N_YZ
    for h in range(heads):
        both = jnp.concatenate([kacc_ref[h] * score_scale, vacc_ref[h]], axis=0)
        both = jnp.transpose(both).astype(BF16)
        lanes = slice(h * 128, (h + 1) * 128)
        keep_ref[:, 0:per, lanes] = both[:half].reshape(N_YZ, per, 128)
        send_ref[:, 0:per, lanes] = both[half:].reshape(N_YZ, per, 128)
    width = link_ref.shape[2]
    lane_iota = lax.broadcasted_iota(jnp.int32, (SPLIT, width), 0).astype(F32).astype(BF16)
    sup_iota = lax.broadcasted_iota(jnp.int32, (width // 2, width), 0)
    one = jnp.ones((), BF16)
    zero = jnp.zeros((), BF16)
    for block in range(link_ref.shape[0]):
        cell = link_ref[block, 0:1, :]
        picked = jnp.zeros((cols, width), F32)
        for part in range(cells // SPLIT):
            low = jnp.where(cell // SPLIT == part, cell % SPLIT, -1).astype(F32).astype(BF16)
            onehot = jnp.where(lane_iota == low, one, zero)
            picked += dot(qg_ref[:, part * SPLIT : (part + 1) * SPLIT], onehot, 1, 0)
        picked = picked.astype(BF16)
        low = jnp.where(sup_iota == link_ref[block, 1:2, :], 1.0, 0.0).astype(BF16)
        high = jnp.where(sup_iota == link_ref[block, 2:3, :], 1.0, 0.0).astype(BF16)
        sums = jnp.concatenate([dot(low, picked, 1, 1), dot(high, picked, 1, 1)], axis=1).astype(BF16)
        per_side = sums.shape[0] // 2
        for side, out_ref in enumerate((keep_ref, send_ref)):
            out_ref[block * GROUP : (block + 1) * GROUP, 16:32, :] = sums[
                side * per_side : (side + 1) * per_side
            ].reshape(GROUP, 16, 2 * cols)


def attention(links, queries, out_grad, mine, other):
    cols, cells = queries.shape
    half = mine.shape[0]
    anchors = 2 * half
    heads = cols // HEAD_DIM
    vmem = pl.BlockSpec(memory_space=pltpu.VMEM)
    payload = jax.ShapeDtypeStruct((N_YZ, 32, 2 * cols), BF16)
    return pl.pallas_call(
        attention_kernel,
        in_specs=[vmem] * 5,
        out_specs=[vmem] * 3,
        out_shape=[jax.ShapeDtypeStruct((cols, cells), BF16), payload, payload],
        scratch_shapes=[
            pltpu.VMEM((heads, anchors, 2 * HEAD_DIM), BF16),
            pltpu.VMEM((heads, anchors, HEAD_DIM), BF16),
            pltpu.VMEM((heads, HEAD_DIM, anchors), BF16),
            pltpu.VMEM((anchors, TILE), F32),
            pltpu.VMEM((anchors, TILE), F32),
            pltpu.VMEM((anchors, TILE), F32),
            pltpu.VMEM((anchors, TILE), F32),
            pltpu.VMEM((anchors, TILE), BF16),
            pltpu.VMEM((anchors, TILE), BF16),
            pltpu.VMEM((heads, HEAD_DIM, anchors), F32),
            pltpu.VMEM((heads, HEAD_DIM, anchors), F32),
        ],
        compiler_params=pltpu.CompilerParams(vmem_limit_bytes=40 << 20),
        name="attention_grad",
    )(links, queries, out_grad, mine, other)


def link_table(link_cell, link_super, link_count, core):
    owners, slots = link_cell.shape
    live = jnp.arange(slots, dtype=jnp.int32)[None, :] < link_count[:, None]
    table = jnp.stack([jnp.where(live, link_cell, -1), jnp.where(live, link_super, -1)], axis=0)
    table = table.reshape(2, owners // N_CORE // GROUP, GROUP, N_CORE, slots)
    table = jnp.where(core == 0, table, table[:, :, :, ::-1])
    table = jnp.transpose(table, (1, 0, 3, 2, 4))
    place = (jnp.arange(N_CORE)[:, None] * GROUP + jnp.arange(GROUP)[None, :])[:, :, None] * 16
    place = place.astype(jnp.int32)
    cell, sup = table[:, 0], table[:, 1]
    low = jnp.where((sup >= 0) & (sup < 16), place + sup, -1)
    high = jnp.where(sup >= 16, place + sup - 16, -1)
    return jnp.stack([cell, low, high], axis=1).reshape(-1, 3, N_CORE * GROUP * slots)


def copies_kernel(keys_ref, values_ref, out_ref):
    pair = jnp.concatenate([keys_ref[...], values_ref[...]], axis=1)
    out_ref[...] = jnp.broadcast_to(pair[None], out_ref.shape)


def copies(keys, values):
    vmem = pl.BlockSpec(memory_space=pltpu.VMEM)
    return pl.pallas_call(
        copies_kernel,
        in_specs=[vmem] * 2,
        out_specs=vmem,
        out_shape=jax.ShapeDtypeStruct((N_YZ, keys.shape[0], 2 * keys.shape[1]), BF16),
        compiler_params=pltpu.CompilerParams(vmem_limit_bytes=8 << 20),
        name="copies",
    )(keys, values)


def final_kernel(part_ref, key_ref, value_ref, super_ref):
    total = jnp.sum(part_ref[...].astype(F32), axis=0)
    anchors = key_ref.shape[0]
    cols = key_ref.shape[1]
    top = total[:anchors]
    for h in range(cols // HEAD_DIM):
        lanes = slice(h * HEAD_DIM, (h + 1) * HEAD_DIM)
        key_ref[:, lanes] = top[:, 2 * h * HEAD_DIM : (2 * h + 1) * HEAD_DIM]
        value_ref[:, lanes] = top[:, (2 * h + 1) * HEAD_DIM : (2 * h + 2) * HEAD_DIM]
    super_ref[0:16, :] = total[anchors:, :cols]
    super_ref[16:32, :] = total[anchors:, cols:]


def final(part, anchors, cols):
    vmem = pl.BlockSpec(memory_space=pltpu.VMEM)
    return pl.pallas_call(
        final_kernel,
        in_specs=[vmem],
        out_specs=[vmem] * 3,
        out_shape=[
            jax.ShapeDtypeStruct((anchors, cols), F32),
            jax.ShapeDtypeStruct((anchors, cols), F32),
            jax.ShapeDtypeStruct((SUP_DEV, cols), F32),
        ],
        compiler_params=pltpu.CompilerParams(vmem_limit_bytes=8 << 20),
        name="final",
    )(part)


def local(queries, anchor_keys, anchor_values, out_grad, link_cell, link_super, link_count):
    cols = queries.shape[0]
    partner = [(i, i ^ 1) for i in range(N_PB)]
    core = lax.axis_index("pb") % N_CORE
    links = link_table(link_cell[0], link_super[0], link_count[0], core)
    spread = copies(anchor_keys, anchor_values)
    mine = lax.all_to_all(spread, "pb", 0, 0, axis_index_groups=pb_groups("yz"), tiled=True)
    mine = mine.reshape(-1, 2 * cols)
    other = lax.ppermute(mine, "pb", partner)
    query_grad, keep, send = attention(links, queries, out_grad, mine, other)

    got = lax.ppermute(send, "pb", partner)
    part = (keep.astype(F32) + got.astype(F32)).astype(BF16)
    part = part.reshape(N_Y, N_Z, 32, 2 * cols)
    part = lax.all_to_all(part, "pb", 0, 0, axis_index_groups=pb_groups("y"), tiled=True)
    part = jnp.sum(part.astype(F32), axis=0).astype(BF16)
    part = lax.all_to_all(part, "pb", 0, 0, axis_index_groups=pb_groups("z"), tiled=True)
    key_grad, value_grad, super_grad = final(part, anchor_keys.shape[0], cols)
    return (query_grad, key_grad, value_grad, super_grad)


def solution(mesh):
    return jax.shard_map(
        local,
        mesh=mesh,
        in_specs=(
            P("sa", "pb"),
            P("pb", "sa"),
            P("pb", "sa"),
            P("sa", "pb"),
            P("pb", None, None),
            P("pb", None, None),
            P("pb", None),
        ),
        out_specs=(P("sa", "pb"), P("pb", "sa"), P("pb", "sa"), P("pb", "sa")),
        check_vma=False,
    )
```

```python
import math

import jax
import jax.numpy as jnp
from jax import lax
from jax.experimental import pallas as pl
from jax.experimental.pallas import tpu as pltpu
from jax.sharding import PartitionSpec as P

HEAD_DIM = 64
SUP_DEV = 32
N_Y, N_Z, N_CORE = 4, 8, 2
N_YZ = N_Y * N_Z
N_PB = N_YZ * N_CORE
TILE = 256
CHUNK = 256
GROUP = N_Z
SPLIT = 256
PAIR = 4
SUB = 256
F32 = jnp.float32
BF16 = jnp.bfloat16


def rank(y, z, c):
    return (y % N_Y * N_Z + z) * N_CORE + c


def pb_groups(axis):
    if axis == "z":
        return [[rank(y, z, c) for z in range(N_Z)] for y in range(N_Y) for c in range(N_CORE)]
    return [[rank(y, z, c) for y in range(N_Y) for z in range(N_Z)] for c in range(N_CORE)]


def y_shift(d):
    return [
        (rank(y, z, c), rank(y + d, z, c))
        for y in range(N_Y)
        for z in range(N_Z)
        for c in range(N_CORE)
    ]


def dot(left, right, left_dim, right_dim):
    return lax.dot_general(
        left, right, (((left_dim,), (right_dim,)), ((), ())), preferred_element_type=F32
    )


def fold(values, op):
    rows, cols = values.shape
    return op(values.reshape(rows // 8, 8, cols), axis=0)


def attention_kernel(
    y_ref, link_ref, q_ref, g_ref, mine_ref, other_ref, qg_ref, keep_ref, send_ref,
    kp_ref, vh_ref, kt_ref, s0_ref, s1_ref, ga0_ref, ga1_ref, p0_ref, p1_ref, kacc_ref, vacc_ref,
):
    cols, cells = q_ref.shape
    heads = cols // HEAD_DIM
    half = mine_ref.shape[0]
    anchors = 2 * half
    tiles = cells // TILE
    units = heads * tiles
    score_scale = HEAD_DIM ** -0.5
    chunks = range(0, anchors, CHUNK)
    bufs = ((s0_ref, ga0_ref, p0_ref), (s1_ref, ga1_ref, p1_ref))

    for part, source in enumerate((mine_ref, other_ref)):
        span = slice(part * half, (part + 1) * half)
        for h in range(heads):
            keys = source[:, h * HEAD_DIM : (h + 1) * HEAD_DIM].astype(F32)
            scaled = keys * (score_scale * math.log2(math.e))
            high = scaled.astype(BF16)
            low = (scaled - high.astype(F32)).astype(BF16)
            kp_ref[h, span, :] = jnp.concatenate([high, low], axis=1)
            vh_ref[h, span, :] = source[:, cols + h * HEAD_DIM : cols + (h + 1) * HEAD_DIM]
            kt_ref[h, :, span] = jnp.transpose(keys * score_scale).astype(BF16)
    kacc_ref[...] = jnp.zeros_like(kacc_ref)
    vacc_ref[...] = jnp.zeros_like(vacc_ref)

    def place(unit):
        head = unit // tiles
        rows = pl.ds(pl.multiple_of(head * HEAD_DIM, HEAD_DIM), HEAD_DIM)
        lanes = pl.ds(pl.multiple_of((unit % tiles) * TILE, TILE), TILE)
        return head, rows, lanes

    def step(unit, slot, top, inverse, delta, first=True, second=True, third=True):
        s_next, _, _ = bufs[slot]
        s_now, ga_now, p_now = bufs[1 - slot]
        _, ga_old, p_old = bufs[slot]
        new_top = new_inverse = new_delta = None
        if first:
            head1, rows1, lanes1 = place(unit)
            q1 = q_ref[rows1, lanes1]
            q1 = jnp.concatenate([q1, q1], axis=0)
        if second:
            head2, rows2, lanes2 = place(unit - 1)
            g2 = g_ref[rows2, lanes2]
            total = jnp.zeros((8, TILE), F32)
            moment = jnp.zeros((8, TILE), F32)
        if third:
            head3, rows3, lanes3 = place(unit - 2)
            q3 = (q_ref[rows3, lanes3].astype(F32) * inverse).astype(BF16)
            g3 = (g_ref[rows3, lanes3].astype(F32) * inverse).astype(BF16)
            qg = jnp.zeros((HEAD_DIM, TILE), F32)
        for a in chunks:
            span = slice(a, a + CHUNK)
            if first:
                for b in range(a, a + CHUNK, SUB):
                    sub = slice(b, b + SUB)
                    part = dot(kp_ref[head1, sub, :], q1, 1, 0)
                    s_next[sub, :] = part
                    part = fold(part, jnp.max)
                    new_top = part if new_top is None else jnp.maximum(new_top, part)
            if second:
                for b in range(a, a + CHUNK, SUB):
                    sub = slice(b, b + SUB)
                    ga = dot(vh_ref[head2, sub, :], g2, 1, 0)
                    p = jnp.exp2(s_now[sub, :] - top)
                    total += fold(p, jnp.sum)
                    moment += fold(p * ga, jnp.sum)
                    p_now[sub, :] = p.astype(BF16)
                    ga_now[sub, :] = ga
            if third:
                p = p_old[span, :]
                ds = p * (ga_old[span, :] - delta).astype(BF16)
                vacc_ref[head3, :, span] += dot(g3, p, 1, 1)
                kacc_ref[head3, :, span] += dot(q3, ds, 1, 1)
                qg += dot(kt_ref[head3, :, span], ds, 1, 0)
        if first:
            new_top = jnp.max(new_top, axis=0, keepdims=True)
        if second:
            new_inverse = 1.0 / jnp.sum(total, axis=0, keepdims=True)
            new_delta = jnp.sum(moment, axis=0, keepdims=True) * new_inverse
        if third:
            qg_ref[rows3, lanes3] = (qg * inverse).astype(BF16)
        return new_top, new_inverse, new_delta

    top, _, _ = step(0, 0, None, None, None, second=False, third=False)
    top, inverse, delta = step(1, 1, top, None, None, third=False)

    def double(i, carry):
        unit = 2 + 2 * i
        carry = step(unit, 0, *carry)
        return step(unit + 1, 1, *carry)

    top, inverse, delta = lax.fori_loop(0, (units - 2) // 2, double, (top, inverse, delta))
    _, inverse, delta = step(units, 0, top, inverse, delta, first=False)
    step(units + 1, 1, None, inverse, delta, first=False, second=False)

    per = half // N_YZ
    for h in range(heads):
        both = jnp.concatenate([kacc_ref[h] * score_scale, vacc_ref[h]], axis=0)
        both = jnp.transpose(both).astype(BF16)
        lanes = slice(h * 128, (h + 1) * 128)
        for y in range(N_Y):
            spot = pl.ds(((y - y_ref[0]) & (N_Y - 1)) * N_Z, N_Z)
            start = y * N_Z * per
            mine = both[start : start + N_Z * per]
            other = both[half + start : half + start + N_Z * per]
            keep_ref[spot, 0:per, lanes] = mine.reshape(N_Z, per, 128)
            send_ref[spot, 0:per, lanes] = other.reshape(N_Z, per, 128)
    width = link_ref.shape[2]
    lane_iota = lax.broadcasted_iota(jnp.int32, (SPLIT, width), 0).astype(F32).astype(BF16)
    sup_iota = lax.broadcasted_iota(jnp.int32, (width // 2, width), 0)
    one = jnp.ones((), BF16)
    zero = jnp.zeros((), BF16)
    blocks = link_ref.shape[0]
    for pair in range(0, blocks, PAIR):
        picked = [jnp.zeros((cols, width), F32) for _ in range(PAIR)]
        for part in range(cells // SPLIT):
            source = qg_ref[:, part * SPLIT : (part + 1) * SPLIT]
            for i in range(PAIR):
                cell = link_ref[pair + i, 0:1, :]
                low = jnp.where(cell // SPLIT == part, cell % SPLIT, -1).astype(F32).astype(BF16)
                picked[i] += dot(source, jnp.where(lane_iota == low, one, zero), 1, 0)
        for i in range(PAIR):
            block = pair + i
            rows = picked[i].astype(BF16)
            low = jnp.where(sup_iota == link_ref[block, 1:2, :], 1.0, 0.0).astype(BF16)
            high = jnp.where(sup_iota == link_ref[block, 2:3, :], 1.0, 0.0).astype(BF16)
            sums = jnp.concatenate([dot(low, rows, 1, 1), dot(high, rows, 1, 1)], axis=1).astype(BF16)
            per_side = sums.shape[0] // 2
            for side, out_ref in enumerate((keep_ref, send_ref)):
                spot = pl.ds(((block - y_ref[0]) & (N_Y - 1)) * N_Z, N_Z)
                out_ref[spot, 16:32, :] = sums[
                    side * per_side : (side + 1) * per_side
                ].reshape(GROUP, 16, 2 * cols)


def attention(y, links, queries, out_grad, mine, other):
    cols, cells = queries.shape
    half = mine.shape[0]
    anchors = 2 * half
    heads = cols // HEAD_DIM
    vmem = pl.BlockSpec(memory_space=pltpu.VMEM)
    payload = jax.ShapeDtypeStruct((N_YZ, 32, 2 * cols), BF16)
    return pl.pallas_call(
        attention_kernel,
        in_specs=[pl.BlockSpec(memory_space=pltpu.SMEM)] + [vmem] * 5,
        out_specs=[vmem] * 3,
        out_shape=[jax.ShapeDtypeStruct((cols, cells), BF16), payload, payload],
        scratch_shapes=[
            pltpu.VMEM((heads, anchors, 2 * HEAD_DIM), BF16),
            pltpu.VMEM((heads, anchors, HEAD_DIM), BF16),
            pltpu.VMEM((heads, HEAD_DIM, anchors), BF16),
            pltpu.VMEM((anchors, TILE), F32),
            pltpu.VMEM((anchors, TILE), F32),
            pltpu.VMEM((anchors, TILE), F32),
            pltpu.VMEM((anchors, TILE), F32),
            pltpu.VMEM((anchors, TILE), BF16),
            pltpu.VMEM((anchors, TILE), BF16),
            pltpu.VMEM((heads, HEAD_DIM, anchors), F32),
            pltpu.VMEM((heads, HEAD_DIM, anchors), F32),
        ],
        compiler_params=pltpu.CompilerParams(vmem_limit_bytes=40 << 20),
        name="attention_grad",
    )(y, links, queries, out_grad, mine, other)


def link_table(link_cell, link_super, link_count, core):
    owners, slots = link_cell.shape
    live = jnp.arange(slots, dtype=jnp.int32)[None, :] < link_count[:, None]
    table = jnp.stack([jnp.where(live, link_cell, -1), jnp.where(live, link_super, -1)], axis=0)
    table = table.reshape(2, owners // N_CORE // GROUP, GROUP, N_CORE, slots)
    table = jnp.where(core == 0, table, table[:, :, :, ::-1])
    table = jnp.transpose(table, (1, 0, 3, 2, 4))
    place = (jnp.arange(N_CORE)[:, None] * GROUP + jnp.arange(GROUP)[None, :])[:, :, None] * 16
    place = place.astype(jnp.int32)
    cell, sup = table[:, 0], table[:, 1]
    low = jnp.where((sup >= 0) & (sup < 16), place + sup, -1)
    high = jnp.where(sup >= 16, place + sup - 16, -1)
    return jnp.stack([cell, low, high], axis=1).reshape(-1, 3, N_CORE * GROUP * slots)


def copies_kernel(keys_hbm, values_hbm, out_ref, keys_ref, values_ref, sems):
    loads = (
        pltpu.make_async_copy(keys_hbm, keys_ref, sems.at[0]),
        pltpu.make_async_copy(values_hbm, values_ref, sems.at[1]),
    )
    for load in loads:
        load.start()
    for load in loads:
        load.wait()
    pair = jnp.concatenate([keys_ref[...], values_ref[...]], axis=1)
    out_ref[...] = jnp.broadcast_to(pair[None], out_ref.shape)


def copies(keys, values):
    hbm = pl.BlockSpec(memory_space=pltpu.HBM)
    return pl.pallas_call(
        copies_kernel,
        in_specs=[hbm] * 2,
        out_specs=pl.BlockSpec(memory_space=pltpu.VMEM),
        out_shape=jax.ShapeDtypeStruct((N_YZ, keys.shape[0], 2 * keys.shape[1]), BF16),
        scratch_shapes=[
            pltpu.VMEM(keys.shape, BF16),
            pltpu.VMEM(values.shape, BF16),
            pltpu.SemaphoreType.DMA((2,)),
        ],
        name="copies",
    )(keys, values)


def final_kernel(part_ref, key_ref, value_ref, super_ref):
    total = jnp.sum(part_ref[...].astype(F32), axis=0)
    anchors = key_ref.shape[0]
    cols = key_ref.shape[1]
    top = total[:anchors]
    for h in range(cols // HEAD_DIM):
        lanes = slice(h * HEAD_DIM, (h + 1) * HEAD_DIM)
        key_ref[:, lanes] = top[:, 2 * h * HEAD_DIM : (2 * h + 1) * HEAD_DIM]
        value_ref[:, lanes] = top[:, (2 * h + 1) * HEAD_DIM : (2 * h + 2) * HEAD_DIM]
    super_ref[0:16, :] = total[anchors:, :cols]
    super_ref[16:32, :] = total[anchors:, cols:]


def final(part, anchors, cols):
    vmem = pl.BlockSpec(memory_space=pltpu.VMEM)
    return pl.pallas_call(
        final_kernel,
        in_specs=[vmem],
        out_specs=[vmem] * 3,
        out_shape=[
            jax.ShapeDtypeStruct((anchors, cols), F32),
            jax.ShapeDtypeStruct((anchors, cols), F32),
            jax.ShapeDtypeStruct((SUP_DEV, cols), F32),
        ],
        compiler_params=pltpu.CompilerParams(vmem_limit_bytes=8 << 20),
        name="final",
    )(part)


def local(queries, anchor_keys, anchor_values, out_grad, link_cell, link_super, link_count):
    cols = queries.shape[0]
    partner = [(i, i ^ 1) for i in range(N_PB)]
    core = lax.axis_index("pb") % N_CORE
    links = link_table(link_cell[0], link_super[0], link_count[0], core)
    spread = copies(anchor_keys, anchor_values)
    mine = lax.all_to_all(spread, "pb", 0, 0, axis_index_groups=pb_groups("yz"), tiled=True)
    mine = mine.reshape(-1, 2 * cols)
    other = lax.ppermute(mine, "pb", partner)
    y = (lax.axis_index("pb") // (N_Z * N_CORE)).astype(jnp.int32).reshape(1)
    query_grad, keep, send = attention(y, links, queries, out_grad, mine, other)

    got = lax.ppermute(send, "pb", partner)
    part = (keep.astype(F32) + got.astype(F32)).astype(BF16).reshape(N_Y, N_Z, 32, 2 * cols)
    parts = [part[0]] + [lax.ppermute(part[d], "pb", y_shift(d)) for d in (2, 1, 3)]
    part = sum(p.astype(F32) for p in parts).astype(BF16)
    part = lax.all_to_all(part, "pb", 0, 0, axis_index_groups=pb_groups("z"), tiled=True)
    key_grad, value_grad, super_grad = final(part, anchor_keys.shape[0], cols)
    return (query_grad, key_grad, value_grad, super_grad)


def solution(mesh):
    return jax.shard_map(
        local,
        mesh=mesh,
        in_specs=(
            P("sa", "pb"),
            P("pb", "sa"),
            P("pb", "sa"),
            P("sa", "pb"),
            P("pb", None, None),
            P("pb", None, None),
            P("pb", None),
        ),
        out_specs=(P("sa", "pb"), P("pb", "sa"), P("pb", "sa"), P("pb", "sa")),
        check_vma=False,
    )
```

```python
import math

import jax
import jax.numpy as jnp
from jax import lax
from jax.experimental import pallas as pl
from jax.experimental.pallas import tpu as pltpu
from jax.sharding import PartitionSpec as P

HEAD_DIM = 64
SUP_DEV = 32
N_Y, N_Z, N_CORE = 4, 8, 2
N_YZ = N_Y * N_Z
N_PB = N_YZ * N_CORE
TILE = 256
CHUNK = 256
GROUP = N_Z
SPLIT = 256
PAIR = 4
SUB = 256
F32 = jnp.float32
BF16 = jnp.bfloat16


def rank(y, z, c):
    return (y % N_Y * N_Z + z) * N_CORE + c


def pb_groups(axis):
    if axis == "z":
        return [[rank(y, z, c) for z in range(N_Z)] for y in range(N_Y) for c in range(N_CORE)]
    return [[rank(y, z, c) for y in range(N_Y) for z in range(N_Z)] for c in range(N_CORE)]


def y_shift(d):
    return [
        (rank(y, z, c), rank(y + d, z, c))
        for y in range(N_Y)
        for z in range(N_Z)
        for c in range(N_CORE)
    ]


def dot(left, right, left_dim, right_dim):
    return lax.dot_general(
        left, right, (((left_dim,), (right_dim,)), ((), ())), preferred_element_type=F32
    )


def fold(values, op):
    rows, cols = values.shape
    return op(values.reshape(rows // 8, 8, cols), axis=0)


def attention_kernel(
    y_ref, link_ref, q_ref, g_ref, mine_ref, other_ref, qg_ref, keep_ref, send_ref,
    kp_ref, vh_ref, kt_ref, s0_ref, s1_ref, ga0_ref, ga1_ref, p0_ref, p1_ref, kacc_ref, vacc_ref,
):
    cols, cells = q_ref.shape
    heads = cols // HEAD_DIM
    half = mine_ref.shape[0]
    anchors = 2 * half
    tiles = cells // TILE
    units = heads * tiles
    score_scale = HEAD_DIM ** -0.5
    chunks = range(0, anchors, CHUNK)
    bufs = ((s0_ref, ga0_ref, p0_ref), (s1_ref, ga1_ref, p1_ref))

    for part, source in enumerate((mine_ref, other_ref)):
        span = slice(part * half, (part + 1) * half)
        for h in range(heads):
            keys = source[:, h * HEAD_DIM : (h + 1) * HEAD_DIM].astype(F32)
            scaled = keys * (score_scale * math.log2(math.e))
            high = scaled.astype(BF16)
            low = (scaled - high.astype(F32)).astype(BF16)
            kp_ref[h, span, :] = jnp.concatenate([high, low], axis=1)
            vh_ref[h, span, :] = source[:, cols + h * HEAD_DIM : cols + (h + 1) * HEAD_DIM]
            kt_ref[h, :, span] = jnp.transpose(keys * score_scale).astype(BF16)
    kacc_ref[...] = jnp.zeros_like(kacc_ref)
    vacc_ref[...] = jnp.zeros_like(vacc_ref)

    def place(unit):
        head = unit // tiles
        rows = pl.ds(pl.multiple_of(head * HEAD_DIM, HEAD_DIM), HEAD_DIM)
        lanes = pl.ds(pl.multiple_of((unit % tiles) * TILE, TILE), TILE)
        return head, rows, lanes

    def step(unit, slot, top, inverse, delta, first=True, second=True, third=True):
        s_next, _, _ = bufs[slot]
        s_now, ga_now, p_now = bufs[1 - slot]
        _, ga_old, p_old = bufs[slot]
        new_top = new_inverse = new_delta = None
        if first:
            head1, rows1, lanes1 = place(unit)
            q1 = q_ref[rows1, lanes1]
            q1 = jnp.concatenate([q1, q1], axis=0)
        if second:
            head2, rows2, lanes2 = place(unit - 1)
            g2 = g_ref[rows2, lanes2]
            total = jnp.zeros((8, TILE), F32)
            moment = jnp.zeros((8, TILE), F32)
        if third:
            head3, rows3, lanes3 = place(unit - 2)
            q3 = (q_ref[rows3, lanes3].astype(F32) * inverse).astype(BF16)
            g3 = (g_ref[rows3, lanes3].astype(F32) * inverse).astype(BF16)
            qg = jnp.zeros((HEAD_DIM, TILE), F32)
        for a in chunks:
            span = slice(a, a + CHUNK)
            if first:
                for b in range(a, a + CHUNK, SUB):
                    sub = slice(b, b + SUB)
                    part = dot(kp_ref[head1, sub, :], q1, 1, 0)
                    s_next[sub, :] = part
                    part = fold(part, jnp.max)
                    new_top = part if new_top is None else jnp.maximum(new_top, part)
            if second:
                for b in range(a, a + CHUNK, SUB):
                    sub = slice(b, b + SUB)
                    ga = dot(vh_ref[head2, sub, :], g2, 1, 0)
                    p = jnp.exp2(s_now[sub, :] - top)
                    total += fold(p, jnp.sum)
                    moment += fold(p * ga, jnp.sum)
                    p_now[sub, :] = p.astype(BF16)
                    ga_now[sub, :] = ga
            if third:
                p = p_old[span, :]
                ds = p * (ga_old[span, :] - delta).astype(BF16)
                vacc_ref[head3, :, span] += dot(g3, p, 1, 1)
                kacc_ref[head3, :, span] += dot(q3, ds, 1, 1)
                qg += dot(kt_ref[head3, :, span], ds, 1, 0)
        if first:
            new_top = jnp.max(new_top, axis=0, keepdims=True)
        if second:
            new_inverse = 1.0 / jnp.sum(total, axis=0, keepdims=True)
            new_delta = jnp.sum(moment, axis=0, keepdims=True) * new_inverse
        if third:
            qg_ref[rows3, lanes3] = (qg * inverse).astype(BF16)
        return new_top, new_inverse, new_delta

    top, _, _ = step(0, 0, None, None, None, second=False, third=False)
    top, inverse, delta = step(1, 1, top, None, None, third=False)

    def double(i, carry):
        unit = 2 + 2 * i
        carry = step(unit, 0, *carry)
        return step(unit + 1, 1, *carry)

    top, inverse, delta = lax.fori_loop(0, (units - 2) // 2, double, (top, inverse, delta))
    _, inverse, delta = step(units, 0, top, inverse, delta, first=False)
    step(units + 1, 1, None, inverse, delta, first=False, second=False)

    per = half // N_YZ
    for h in range(heads):
        both = jnp.concatenate([kacc_ref[h] * score_scale, vacc_ref[h]], axis=0)
        both = jnp.transpose(both).astype(BF16)
        lanes = slice(h * 128, (h + 1) * 128)
        for y in range(N_Y):
            spot = pl.ds(y * N_Z, N_Z)
            start = y * N_Z * per
            mine = both[start : start + N_Z * per]
            other = both[half + start : half + start + N_Z * per]
            keep_ref[spot, 0:per, lanes] = mine.reshape(N_Z, per, 128)
            send_ref[spot, 0:per, lanes] = other.reshape(N_Z, per, 128)
    width = link_ref.shape[2]
    lane_iota = lax.broadcasted_iota(jnp.int32, (SPLIT, width), 0).astype(F32).astype(BF16)
    sup_iota = lax.broadcasted_iota(jnp.int32, (width // 2, width), 0)
    one = jnp.ones((), BF16)
    zero = jnp.zeros((), BF16)
    blocks = link_ref.shape[0]
    for pair in range(0, blocks, PAIR):
        picked = [jnp.zeros((cols, width), F32) for _ in range(PAIR)]
        for part in range(cells // SPLIT):
            source = qg_ref[:, part * SPLIT : (part + 1) * SPLIT]
            for i in range(PAIR):
                cell = link_ref[pair + i, 0:1, :]
                low = jnp.where(cell // SPLIT == part, cell % SPLIT, -1).astype(F32).astype(BF16)
                picked[i] += dot(source, jnp.where(lane_iota == low, one, zero), 1, 0)
        for i in range(PAIR):
            block = pair + i
            rows = picked[i].astype(BF16)
            low = jnp.where(sup_iota == link_ref[block, 1:2, :], 1.0, 0.0).astype(BF16)
            high = jnp.where(sup_iota == link_ref[block, 2:3, :], 1.0, 0.0).astype(BF16)
            sums = jnp.concatenate([dot(low, rows, 1, 1), dot(high, rows, 1, 1)], axis=1).astype(BF16)
            per_side = sums.shape[0] // 2
            for side, out_ref in enumerate((keep_ref, send_ref)):
                spot = pl.ds(((block - y_ref[0]) & (N_Y - 1)) * N_Z, N_Z)
                out_ref[spot, 16:32, :] = sums[
                    side * per_side : (side + 1) * per_side
                ].reshape(GROUP, 16, 2 * cols)


def attention(y, links, queries, out_grad, mine, other):
    cols, cells = queries.shape
    half = mine.shape[0]
    anchors = 2 * half
    heads = cols // HEAD_DIM
    vmem = pl.BlockSpec(memory_space=pltpu.VMEM)
    payload = jax.ShapeDtypeStruct((N_YZ, 32, 2 * cols), BF16)
    return pl.pallas_call(
        attention_kernel,
        in_specs=[pl.BlockSpec(memory_space=pltpu.SMEM)] + [vmem] * 5,
        out_specs=[vmem] * 3,
        out_shape=[jax.ShapeDtypeStruct((cols, cells), BF16), payload, payload],
        scratch_shapes=[
            pltpu.VMEM((heads, anchors, 2 * HEAD_DIM), BF16),
            pltpu.VMEM((heads, anchors, HEAD_DIM), BF16),
            pltpu.VMEM((heads, HEAD_DIM, anchors), BF16),
            pltpu.VMEM((anchors, TILE), F32),
            pltpu.VMEM((anchors, TILE), F32),
            pltpu.VMEM((anchors, TILE), F32),
            pltpu.VMEM((anchors, TILE), F32),
            pltpu.VMEM((anchors, TILE), BF16),
            pltpu.VMEM((anchors, TILE), BF16),
            pltpu.VMEM((heads, HEAD_DIM, anchors), F32),
            pltpu.VMEM((heads, HEAD_DIM, anchors), F32),
        ],
        compiler_params=pltpu.CompilerParams(vmem_limit_bytes=40 << 20),
        name="attention_grad",
    )(y, links, queries, out_grad, mine, other)


def link_table(link_cell, link_super, link_count, core):
    owners, slots = link_cell.shape
    live = jnp.arange(slots, dtype=jnp.int32)[None, :] < link_count[:, None]
    table = jnp.stack([jnp.where(live, link_cell, -1), jnp.where(live, link_super, -1)], axis=0)
    table = table.reshape(2, owners // N_CORE // GROUP, GROUP, N_CORE, slots)
    table = jnp.where(core == 0, table, table[:, :, :, ::-1])
    table = jnp.transpose(table, (1, 0, 3, 2, 4))
    place = (jnp.arange(N_CORE)[:, None] * GROUP + jnp.arange(GROUP)[None, :])[:, :, None] * 16
    place = place.astype(jnp.int32)
    cell, sup = table[:, 0], table[:, 1]
    low = jnp.where((sup >= 0) & (sup < 16), place + sup, -1)
    high = jnp.where(sup >= 16, place + sup - 16, -1)
    return jnp.stack([cell, low, high], axis=1).reshape(-1, 3, N_CORE * GROUP * slots)


def copies_kernel(keys_hbm, values_hbm, out_ref, keys_ref, values_ref, sems):
    loads = (
        pltpu.make_async_copy(keys_hbm, keys_ref, sems.at[0]),
        pltpu.make_async_copy(values_hbm, values_ref, sems.at[1]),
    )
    for load in loads:
        load.start()
    for load in loads:
        load.wait()
    pair = jnp.concatenate([keys_ref[...], values_ref[...]], axis=1)
    out_ref[...] = jnp.broadcast_to(pair[None], out_ref.shape)


def copies(keys, values):
    hbm = pl.BlockSpec(memory_space=pltpu.HBM)
    return pl.pallas_call(
        copies_kernel,
        in_specs=[hbm] * 2,
        out_specs=pl.BlockSpec(memory_space=pltpu.VMEM),
        out_shape=jax.ShapeDtypeStruct((N_Z, keys.shape[0], 2 * keys.shape[1]), BF16),
        scratch_shapes=[
            pltpu.VMEM(keys.shape, BF16),
            pltpu.VMEM(values.shape, BF16),
            pltpu.SemaphoreType.DMA((2,)),
        ],
        name="copies",
    )(keys, values)


def final_kernel(part_ref, key_ref, value_ref, super_ref):
    total = jnp.sum(part_ref[...].astype(F32), axis=0)
    anchors = key_ref.shape[0]
    cols = key_ref.shape[1]
    top = total[:anchors]
    for h in range(cols // HEAD_DIM):
        lanes = slice(h * HEAD_DIM, (h + 1) * HEAD_DIM)
        key_ref[:, lanes] = top[:, 2 * h * HEAD_DIM : (2 * h + 1) * HEAD_DIM]
        value_ref[:, lanes] = top[:, (2 * h + 1) * HEAD_DIM : (2 * h + 2) * HEAD_DIM]
    super_ref[0:16, :] = total[anchors:, :cols]
    super_ref[16:32, :] = total[anchors:, cols:]


def final(part, anchors, cols):
    vmem = pl.BlockSpec(memory_space=pltpu.VMEM)
    return pl.pallas_call(
        final_kernel,
        in_specs=[vmem],
        out_specs=[vmem] * 3,
        out_shape=[
            jax.ShapeDtypeStruct((anchors, cols), F32),
            jax.ShapeDtypeStruct((anchors, cols), F32),
            jax.ShapeDtypeStruct((SUP_DEV, cols), F32),
        ],
        compiler_params=pltpu.CompilerParams(vmem_limit_bytes=8 << 20),
        name="final",
    )(part)


def local(queries, anchor_keys, anchor_values, out_grad, link_cell, link_super, link_count):
    cols = queries.shape[0]
    partner = [(i, i ^ 1) for i in range(N_PB)]
    core = lax.axis_index("pb") % N_CORE
    links = link_table(link_cell[0], link_super[0], link_count[0], core)
    spread = copies(anchor_keys, anchor_values)
    row = lax.all_to_all(spread, "pb", 0, 0, axis_index_groups=pb_groups("z"), tiled=True)
    rows = {d: lax.ppermute(row, "pb", y_shift(-d)) for d in (1, 3, 2)}
    mine = jnp.stack([row, rows[1], rows[2], rows[3]]).reshape(-1, 2 * cols)
    other = lax.ppermute(mine, "pb", partner)
    y = (lax.axis_index("pb") // (N_Z * N_CORE)).astype(jnp.int32).reshape(1)
    query_grad, keep, send = attention(y, links, queries, out_grad, mine, other)

    got = lax.ppermute(send, "pb", partner)
    part = (keep.astype(F32) + got.astype(F32)).astype(BF16).reshape(N_Y, N_Z, 32, 2 * cols)
    parts = [part[0]] + [lax.ppermute(part[d], "pb", y_shift(d)) for d in (2, 1, 3)]
    part = sum(p.astype(F32) for p in parts).astype(BF16)
    part = lax.all_to_all(part, "pb", 0, 0, axis_index_groups=pb_groups("z"), tiled=True)
    key_grad, value_grad, super_grad = final(part, anchor_keys.shape[0], cols)
    return (query_grad, key_grad, value_grad, super_grad)


def solution(mesh):
    return jax.shard_map(
        local,
        mesh=mesh,
        in_specs=(
            P("sa", "pb"),
            P("pb", "sa"),
            P("pb", "sa"),
            P("sa", "pb"),
            P("pb", None, None),
            P("pb", None, None),
            P("pb", None),
        ),
        out_specs=(P("sa", "pb"), P("pb", "sa"), P("pb", "sa"), P("pb", "sa")),
        check_vma=False,
    )
```

```python
import math

import jax
import jax.numpy as jnp
from jax import lax
from jax.experimental import pallas as pl
from jax.experimental.pallas import tpu as pltpu
from jax.sharding import PartitionSpec as P

HEAD_DIM = 64
SUP_DEV = 32
N_Y, N_Z, N_CORE = 4, 8, 2
N_YZ = N_Y * N_Z
N_PB = N_YZ * N_CORE
TILE = 256
CHUNK = 256
GROUP = N_Z
SPLIT = 256
PAIR = 4
SUB = 256
F32 = jnp.float32
BF16 = jnp.bfloat16


def rank(y, z, c):
    return (y % N_Y * N_Z + z) * N_CORE + c


def pb_groups(axis):
    if axis == "z":
        return [[rank(y, z, c) for z in range(N_Z)] for y in range(N_Y) for c in range(N_CORE)]
    return [[rank(y, z, c) for y in range(N_Y) for z in range(N_Z)] for c in range(N_CORE)]


def y_shift(d):
    return [
        (rank(y, z, c), rank(y + d, z, c))
        for y in range(N_Y)
        for z in range(N_Z)
        for c in range(N_CORE)
    ]


def dot(left, right, left_dim, right_dim):
    return lax.dot_general(
        left, right, (((left_dim,), (right_dim,)), ((), ())), preferred_element_type=F32
    )


def fold(values, op):
    rows, cols = values.shape
    return op(values.reshape(rows // 8, 8, cols), axis=0)


def attention_kernel(
    y_ref, link_ref, q_ref, g_ref, mine_ref, other_ref, qg_ref, keep_ref, send_ref,
    kp_ref, vh_ref, kt_ref, s0_ref, s1_ref, ga0_ref, ga1_ref, p0_ref, p1_ref, kacc_ref, vacc_ref,
):
    cols, cells = q_ref.shape
    heads = cols // HEAD_DIM
    half = mine_ref.shape[0]
    anchors = 2 * half
    tiles = cells // TILE
    units = heads * tiles
    score_scale = HEAD_DIM ** -0.5
    chunks = range(0, anchors, CHUNK)
    bufs = ((s0_ref, ga0_ref, p0_ref), (s1_ref, ga1_ref, p1_ref))

    for part, source in enumerate((mine_ref, other_ref)):
        span = slice(part * half, (part + 1) * half)
        for h in range(heads):
            keys = source[:, h * HEAD_DIM : (h + 1) * HEAD_DIM].astype(F32)
            scaled = keys * (score_scale * math.log2(math.e))
            high = scaled.astype(BF16)
            low = (scaled - high.astype(F32)).astype(BF16)
            kp_ref[h, span, :] = jnp.concatenate([high, low], axis=1)
            vh_ref[h, span, :] = source[:, cols + h * HEAD_DIM : cols + (h + 1) * HEAD_DIM]
            kt_ref[h, :, span] = jnp.transpose(keys * score_scale).astype(BF16)
    kacc_ref[...] = jnp.zeros_like(kacc_ref)
    vacc_ref[...] = jnp.zeros_like(vacc_ref)

    def place(unit):
        head = unit // tiles
        rows = pl.ds(pl.multiple_of(head * HEAD_DIM, HEAD_DIM), HEAD_DIM)
        lanes = pl.ds(pl.multiple_of((unit % tiles) * TILE, TILE), TILE)
        return head, rows, lanes

    def step(unit, slot, top, inverse, delta, first=True, second=True, third=True):
        s_next, _, _ = bufs[slot]
        s_now, ga_now, p_now = bufs[1 - slot]
        _, ga_old, p_old = bufs[slot]
        new_top = new_inverse = new_delta = None
        if first:
            head1, rows1, lanes1 = place(unit)
            q1 = q_ref[rows1, lanes1]
            q1 = jnp.concatenate([q1, q1], axis=0)
        if second:
            head2, rows2, lanes2 = place(unit - 1)
            g2 = g_ref[rows2, lanes2]
            total = jnp.zeros((8, TILE), F32)
            moment = jnp.zeros((8, TILE), F32)
        if third:
            head3, rows3, lanes3 = place(unit - 2)
            q3 = (q_ref[rows3, lanes3].astype(F32) * inverse).astype(BF16)
            g3 = (g_ref[rows3, lanes3].astype(F32) * inverse).astype(BF16)
            qg = jnp.zeros((HEAD_DIM, TILE), F32)
        for a in chunks:
            span = slice(a, a + CHUNK)
            if first:
                for b in range(a, a + CHUNK, SUB):
                    sub = slice(b, b + SUB)
                    part = dot(kp_ref[head1, sub, :], q1, 1, 0)
                    s_next[sub, :] = part
                    part = fold(part, jnp.max)
                    new_top = part if new_top is None else jnp.maximum(new_top, part)
            if second:
                for b in range(a, a + CHUNK, SUB):
                    sub = slice(b, b + SUB)
                    ga = dot(vh_ref[head2, sub, :], g2, 1, 0)
                    p = jnp.exp2(s_now[sub, :] - top)
                    total += fold(p, jnp.sum)
                    moment += fold(p * ga, jnp.sum)
                    p_now[sub, :] = p.astype(BF16)
                    ga_now[sub, :] = ga
            if third:
                p = p_old[span, :]
                ds = p * (ga_old[span, :] - delta).astype(BF16)
                vacc_ref[head3, :, span] += dot(g3, p, 1, 1)
                kacc_ref[head3, :, span] += dot(q3, ds, 1, 1)
                qg += dot(kt_ref[head3, :, span], ds, 1, 0)
        if first:
            new_top = jnp.max(new_top, axis=0, keepdims=True)
        if second:
            new_inverse = 1.0 / jnp.sum(total, axis=0, keepdims=True)
            new_delta = jnp.sum(moment, axis=0, keepdims=True) * new_inverse
        if third:
            qg_ref[rows3, lanes3] = (qg * inverse).astype(BF16)
        return new_top, new_inverse, new_delta

    top, _, _ = step(0, 0, None, None, None, second=False, third=False)
    top, inverse, delta = step(1, 1, top, None, None, third=False)

    def double(i, carry):
        unit = 2 + 2 * i
        carry = step(unit, 0, *carry)
        return step(unit + 1, 1, *carry)

    top, inverse, delta = lax.fori_loop(0, (units - 2) // 2, double, (top, inverse, delta))
    _, inverse, delta = step(units, 0, top, inverse, delta, first=False)
    step(units + 1, 1, None, inverse, delta, first=False, second=False)

    per = half // N_YZ
    for h in range(heads):
        both = jnp.concatenate([kacc_ref[h] * score_scale, vacc_ref[h]], axis=0)
        both = jnp.transpose(both.astype(BF16))
        lanes = slice(h * 128, (h + 1) * 128)
        for y in range(N_Y):
            spot = pl.ds(y * N_Z, N_Z)
            start = y * N_Z * per
            mine = both[start : start + N_Z * per]
            other = both[half + start : half + start + N_Z * per]
            keep_ref[spot, 0:per, lanes] = mine.reshape(N_Z, per, 128)
            send_ref[spot, 0:per, lanes] = other.reshape(N_Z, per, 128)
    width = link_ref.shape[2]
    lane_iota = lax.broadcasted_iota(jnp.int32, (SPLIT, width), 0).astype(F32).astype(BF16)
    sup_iota = lax.broadcasted_iota(jnp.int32, (width // 2, width), 0)
    one = jnp.ones((), BF16)
    zero = jnp.zeros((), BF16)
    blocks = link_ref.shape[0]
    for pair in range(0, blocks, PAIR):
        picked = [jnp.zeros((cols, width), F32) for _ in range(PAIR)]
        for part in range(cells // SPLIT):
            source = qg_ref[:, part * SPLIT : (part + 1) * SPLIT]
            for i in range(PAIR):
                cell = link_ref[pair + i, 0:1, :]
                low = jnp.where(cell // SPLIT == part, cell % SPLIT, -1).astype(F32).astype(BF16)
                picked[i] += dot(source, jnp.where(lane_iota == low, one, zero), 1, 0)
        for i in range(PAIR):
            block = pair + i
            rows = picked[i].astype(BF16)
            low = jnp.where(sup_iota == link_ref[block, 1:2, :], 1.0, 0.0).astype(BF16)
            high = jnp.where(sup_iota == link_ref[block, 2:3, :], 1.0, 0.0).astype(BF16)
            sums = jnp.concatenate([dot(low, rows, 1, 1), dot(high, rows, 1, 1)], axis=1).astype(BF16)
            per_side = sums.shape[0] // 2
            for side, out_ref in enumerate((keep_ref, send_ref)):
                spot = pl.ds(((block - y_ref[0]) & (N_Y - 1)) * N_Z, N_Z)
                out_ref[spot, 16:32, :] = sums[
                    side * per_side : (side + 1) * per_side
                ].reshape(GROUP, 16, 2 * cols)


def attention(y, links, queries, out_grad, mine, other):
    cols, cells = queries.shape
    half = mine.shape[0]
    anchors = 2 * half
    heads = cols // HEAD_DIM
    vmem = pl.BlockSpec(memory_space=pltpu.VMEM)
    payload = jax.ShapeDtypeStruct((N_YZ, 32, 2 * cols), BF16)
    return pl.pallas_call(
        attention_kernel,
        in_specs=[pl.BlockSpec(memory_space=pltpu.SMEM)] + [vmem] * 5,
        out_specs=[vmem] * 3,
        out_shape=[jax.ShapeDtypeStruct((cols, cells), BF16), payload, payload],
        scratch_shapes=[
            pltpu.VMEM((heads, anchors, 2 * HEAD_DIM), BF16),
            pltpu.VMEM((heads, anchors, HEAD_DIM), BF16),
            pltpu.VMEM((heads, HEAD_DIM, anchors), BF16),
            pltpu.VMEM((anchors, TILE), F32),
            pltpu.VMEM((anchors, TILE), F32),
            pltpu.VMEM((anchors, TILE), F32),
            pltpu.VMEM((anchors, TILE), F32),
            pltpu.VMEM((anchors, TILE), BF16),
            pltpu.VMEM((anchors, TILE), BF16),
            pltpu.VMEM((heads, HEAD_DIM, anchors), F32),
            pltpu.VMEM((heads, HEAD_DIM, anchors), F32),
        ],
        compiler_params=pltpu.CompilerParams(vmem_limit_bytes=40 << 20),
        name="attention_grad",
    )(y, links, queries, out_grad, mine, other)


def link_table(link_cell, link_super, link_count, core):
    owners, slots = link_cell.shape
    live = jnp.arange(slots, dtype=jnp.int32)[None, :] < link_count[:, None]
    table = jnp.stack([jnp.where(live, link_cell, -1), jnp.where(live, link_super, -1)], axis=0)
    table = table.reshape(2, owners // N_CORE // GROUP, GROUP, N_CORE, slots)
    table = jnp.where(core == 0, table, table[:, :, :, ::-1])
    table = jnp.transpose(table, (1, 0, 3, 2, 4))
    place = (jnp.arange(N_CORE)[:, None] * GROUP + jnp.arange(GROUP)[None, :])[:, :, None] * 16
    place = place.astype(jnp.int32)
    cell, sup = table[:, 0], table[:, 1]
    low = jnp.where((sup >= 0) & (sup < 16), place + sup, -1)
    high = jnp.where(sup >= 16, place + sup - 16, -1)
    return jnp.stack([cell, low, high], axis=1).reshape(-1, 3, N_CORE * GROUP * slots)


def copies_kernel(keys_hbm, values_hbm, out_ref, keys_ref, values_ref, sems):
    loads = (
        pltpu.make_async_copy(keys_hbm, keys_ref, sems.at[0]),
        pltpu.make_async_copy(values_hbm, values_ref, sems.at[1]),
    )
    for load in loads:
        load.start()
    for load in loads:
        load.wait()
    pair = jnp.concatenate([keys_ref[...], values_ref[...]], axis=1)
    out_ref[...] = jnp.broadcast_to(pair[None], out_ref.shape)


def copies(keys, values):
    hbm = pl.BlockSpec(memory_space=pltpu.HBM)
    return pl.pallas_call(
        copies_kernel,
        in_specs=[hbm] * 2,
        out_specs=pl.BlockSpec(memory_space=pltpu.VMEM),
        out_shape=jax.ShapeDtypeStruct((N_Z, keys.shape[0], 2 * keys.shape[1]), BF16),
        scratch_shapes=[
            pltpu.VMEM(keys.shape, BF16),
            pltpu.VMEM(values.shape, BF16),
            pltpu.SemaphoreType.DMA((2,)),
        ],
        name="copies",
    )(keys, values)


def final_kernel(part_ref, key_ref, value_ref, super_ref):
    total = jnp.sum(part_ref[...].astype(F32), axis=0)
    anchors = key_ref.shape[0]
    cols = key_ref.shape[1]
    top = total[:anchors]
    for h in range(cols // HEAD_DIM):
        lanes = slice(h * HEAD_DIM, (h + 1) * HEAD_DIM)
        key_ref[:, lanes] = top[:, 2 * h * HEAD_DIM : (2 * h + 1) * HEAD_DIM]
        value_ref[:, lanes] = top[:, (2 * h + 1) * HEAD_DIM : (2 * h + 2) * HEAD_DIM]
    super_ref[0:16, :] = total[anchors:, :cols]
    super_ref[16:32, :] = total[anchors:, cols:]


def final(part, anchors, cols):
    vmem = pl.BlockSpec(memory_space=pltpu.VMEM)
    return pl.pallas_call(
        final_kernel,
        in_specs=[vmem],
        out_specs=[vmem] * 3,
        out_shape=[
            jax.ShapeDtypeStruct((anchors, cols), F32),
            jax.ShapeDtypeStruct((anchors, cols), F32),
            jax.ShapeDtypeStruct((SUP_DEV, cols), F32),
        ],
        compiler_params=pltpu.CompilerParams(vmem_limit_bytes=8 << 20),
        name="final",
    )(part)


def local(queries, anchor_keys, anchor_values, out_grad, link_cell, link_super, link_count):
    cols = queries.shape[0]
    partner = [(i, i ^ 1) for i in range(N_PB)]
    core = lax.axis_index("pb") % N_CORE
    links = link_table(link_cell[0], link_super[0], link_count[0], core)
    spread = copies(anchor_keys, anchor_values)
    row = lax.all_to_all(spread, "pb", 0, 0, axis_index_groups=pb_groups("z"), tiled=True)
    rows = {d: lax.ppermute(row, "pb", y_shift(-d)) for d in (1, 3, 2)}
    mine = jnp.stack([row, rows[1], rows[2], rows[3]]).reshape(-1, 2 * cols)
    other = lax.ppermute(mine, "pb", partner)
    y = (lax.axis_index("pb") // (N_Z * N_CORE)).astype(jnp.int32).reshape(1)
    query_grad, keep, send = attention(y, links, queries, out_grad, mine, other)

    got = lax.ppermute(send, "pb", partner)
    part = (keep.astype(F32) + got.astype(F32)).astype(BF16).reshape(N_Y, N_Z, 32, 2 * cols)
    parts = [part[0]] + [lax.ppermute(part[d], "pb", y_shift(d)) for d in (2, 1, 3)]
    part = sum(p.astype(F32) for p in parts).astype(BF16)
    part = lax.all_to_all(part, "pb", 0, 0, axis_index_groups=pb_groups("z"), tiled=True)
    key_grad, value_grad, super_grad = final(part, anchor_keys.shape[0], cols)
    return (query_grad, key_grad, value_grad, super_grad)


def solution(mesh):
    return jax.shard_map(
        local,
        mesh=mesh,
        in_specs=(
            P("sa", "pb"),
            P("pb", "sa"),
            P("pb", "sa"),
            P("sa", "pb"),
            P("pb", None, None),
            P("pb", None, None),
            P("pb", None),
        ),
        out_specs=(P("sa", "pb"), P("pb", "sa"), P("pb", "sa"), P("pb", "sa")),
        check_vma=False,
    )
```

```python
import math

import jax
import jax.numpy as jnp
from jax import lax
from jax.experimental import pallas as pl
from jax.experimental.pallas import tpu as pltpu
from jax.sharding import PartitionSpec as P

HEAD_DIM = 64
SUP_DEV = 32
N_Y, N_Z, N_CORE = 4, 8, 2
N_YZ = N_Y * N_Z
N_PB = N_YZ * N_CORE
TILE = 256
CHUNK = 256
GROUP = N_Z
SPLIT = 256
PAIR = 4
SUB = 256
F32 = jnp.float32
BF16 = jnp.bfloat16


def rank(y, z, c):
    return (y % N_Y * N_Z + z) * N_CORE + c


def pb_groups(axis):
    if axis == "z":
        return [[rank(y, z, c) for z in range(N_Z)] for y in range(N_Y) for c in range(N_CORE)]
    return [[rank(y, z, c) for y in range(N_Y) for z in range(N_Z)] for c in range(N_CORE)]


def y_shift(d):
    return [
        (rank(y, z, c), rank(y + d, z, c))
        for y in range(N_Y)
        for z in range(N_Z)
        for c in range(N_CORE)
    ]


def dot(left, right, left_dim, right_dim):
    return lax.dot_general(
        left, right, (((left_dim,), (right_dim,)), ((), ())), preferred_element_type=F32
    )


def fold(values, op):
    rows, cols = values.shape
    return op(values.reshape(rows // 8, 8, cols), axis=0)


def attention_kernel(
    y_ref, link_ref, q_ref, g_ref, mine_ref, other_ref, qg_ref, keep_ref, send_ref,
    kp_ref, vh_ref, kt_ref, s0_ref, s1_ref, ga0_ref, ga1_ref, p0_ref, p1_ref, kacc_ref, vacc_ref,
):
    cols, cells = q_ref.shape
    heads = cols // HEAD_DIM
    half = mine_ref.shape[0]
    anchors = 2 * half
    tiles = cells // TILE
    units = heads * tiles
    score_scale = HEAD_DIM ** -0.5
    chunks = range(0, anchors, CHUNK)
    bufs = ((s0_ref, ga0_ref, p0_ref), (s1_ref, ga1_ref, p1_ref))

    for part, source in enumerate((mine_ref, other_ref)):
        span = slice(part * half, (part + 1) * half)
        for h in range(heads):
            keys = source[:, h * HEAD_DIM : (h + 1) * HEAD_DIM].astype(F32)
            scaled = keys * (score_scale * math.log2(math.e))
            high = scaled.astype(BF16)
            low = (scaled - high.astype(F32)).astype(BF16)
            kp_ref[h, span, :] = jnp.concatenate([high, low], axis=1)
            vh_ref[h, span, :] = source[:, cols + h * HEAD_DIM : cols + (h + 1) * HEAD_DIM]
            kt_ref[h, :, span] = jnp.transpose(keys * score_scale).astype(BF16)
    kacc_ref[...] = jnp.zeros_like(kacc_ref)
    vacc_ref[...] = jnp.zeros_like(vacc_ref)

    def place(unit):
        head = unit // tiles
        rows = pl.ds(pl.multiple_of(head * HEAD_DIM, HEAD_DIM), HEAD_DIM)
        lanes = pl.ds(pl.multiple_of((unit % tiles) * TILE, TILE), TILE)
        return head, rows, lanes

    def step(unit, slot, top, inverse, delta, first=True, second=True, third=True):
        s_next, _, _ = bufs[slot]
        s_now, ga_now, p_now = bufs[1 - slot]
        _, ga_old, p_old = bufs[slot]
        new_top = new_inverse = new_delta = None
        if first:
            head1, rows1, lanes1 = place(unit)
            q1 = q_ref[rows1, lanes1]
            q1 = jnp.concatenate([q1, q1], axis=0)
        if second:
            head2, rows2, lanes2 = place(unit - 1)
            g2 = g_ref[rows2, lanes2]
            total = jnp.zeros((8, TILE), F32)
            moment = jnp.zeros((8, TILE), F32)
        if third:
            head3, rows3, lanes3 = place(unit - 2)
            q3 = (q_ref[rows3, lanes3].astype(F32) * inverse).astype(BF16)
            g3 = (g_ref[rows3, lanes3].astype(F32) * inverse).astype(BF16)
            qg = jnp.zeros((HEAD_DIM, TILE), F32)
        for a in chunks:
            span = slice(a, a + CHUNK)
            if first:
                for b in range(a, a + CHUNK, SUB):
                    sub = slice(b, b + SUB)
                    part = dot(kp_ref[head1, sub, :], q1, 1, 0)
                    s_next[sub, :] = part
                    part = fold(part, jnp.max)
                    new_top = part if new_top is None else jnp.maximum(new_top, part)
            if second:
                for b in range(a, a + CHUNK, SUB):
                    sub = slice(b, b + SUB)
                    ga = dot(vh_ref[head2, sub, :], g2, 1, 0)
                    p = jnp.exp2(s_now[sub, :] - top)
                    total += fold(p, jnp.sum)
                    moment += fold(p * ga, jnp.sum)
                    p_now[sub, :] = p.astype(BF16)
                    ga_now[sub, :] = ga
            if third:
                p = p_old[span, :]
                ds = p * (ga_old[span, :] - delta).astype(BF16)
                vacc_ref[head3, :, span] += dot(g3, p, 1, 1)
                kacc_ref[head3, :, span] += dot(q3, ds, 1, 1)
                qg += dot(kt_ref[head3, :, span], ds, 1, 0)
        if first:
            new_top = jnp.max(new_top, axis=0, keepdims=True)
        if second:
            new_inverse = 1.0 / jnp.sum(total, axis=0, keepdims=True)
            new_delta = jnp.sum(moment, axis=0, keepdims=True) * new_inverse
        if third:
            qg_ref[rows3, lanes3] = (qg * inverse).astype(BF16)
        return new_top, new_inverse, new_delta

    top, _, _ = step(0, 0, None, None, None, second=False, third=False)
    top, inverse, delta = step(1, 1, top, None, None, third=False)

    def double(i, carry):
        unit = 2 + 2 * i
        carry = step(unit, 0, *carry)
        return step(unit + 1, 1, *carry)

    top, inverse, delta = lax.fori_loop(0, (units - 2) // 2, double, (top, inverse, delta))
    _, inverse, delta = step(units, 0, top, inverse, delta, first=False)
    step(units + 1, 1, None, inverse, delta, first=False, second=False)

    per = half // N_YZ
    for h in range(heads):
        both = jnp.concatenate([kacc_ref[h] * score_scale, vacc_ref[h]], axis=0)
        both = jnp.transpose(both.astype(BF16))
        lanes = slice(h * 128, (h + 1) * 128)
        for y in range(N_Y):
            spot = pl.ds(y * N_Z, N_Z)
            start = y * N_Z * per
            mine = both[start : start + N_Z * per]
            other = both[half + start : half + start + N_Z * per]
            keep_ref[spot, 0:per, lanes] = mine.reshape(N_Z, per, 128)
            send_ref[spot, 0:per, lanes] = other.reshape(N_Z, per, 128)
    width = link_ref.shape[2]
    lane_iota = lax.broadcasted_iota(jnp.int32, (SPLIT, width), 0).astype(F32).astype(BF16)
    sup_iota = lax.broadcasted_iota(jnp.int32, (width // 2, width), 0)
    one = jnp.ones((), BF16)
    zero = jnp.zeros((), BF16)
    blocks = link_ref.shape[0]
    for pair in range(0, blocks, PAIR):
        picked = [jnp.zeros((cols, width), F32) for _ in range(PAIR)]
        for part in range(cells // SPLIT):
            source = qg_ref[:, part * SPLIT : (part + 1) * SPLIT]
            for i in range(PAIR):
                cell = link_ref[pair + i, 0:1, :]
                low = jnp.where(cell // SPLIT == part, cell % SPLIT, -1).astype(F32).astype(BF16)
                picked[i] += dot(source, jnp.where(lane_iota == low, one, zero), 1, 0)
        for i in range(PAIR):
            block = pair + i
            rows = picked[i].astype(BF16)
            low = jnp.where(sup_iota == link_ref[block, 1:2, :], 1.0, 0.0).astype(BF16)
            high = jnp.where(sup_iota == link_ref[block, 2:3, :], 1.0, 0.0).astype(BF16)
            sums = jnp.concatenate([dot(low, rows, 1, 1), dot(high, rows, 1, 1)], axis=1).astype(BF16)
            per_side = sums.shape[0] // 2
            for side, out_ref in enumerate((keep_ref, send_ref)):
                spot = pl.ds(((block - y_ref[0]) & (N_Y - 1)) * N_Z, N_Z)
                out_ref[spot, 16:32, :] = sums[
                    side * per_side : (side + 1) * per_side
                ].reshape(GROUP, 16, 2 * cols)


def attention(y, links, queries, out_grad, mine, other):
    cols, cells = queries.shape
    half = mine.shape[0]
    anchors = 2 * half
    heads = cols // HEAD_DIM
    vmem = pl.BlockSpec(memory_space=pltpu.VMEM)
    payload = jax.ShapeDtypeStruct((N_YZ, 32, 2 * cols), BF16)
    return pl.pallas_call(
        attention_kernel,
        in_specs=[pl.BlockSpec(memory_space=pltpu.SMEM)] + [vmem] * 5,
        out_specs=[vmem] * 3,
        out_shape=[jax.ShapeDtypeStruct((cols, cells), BF16), payload, payload],
        scratch_shapes=[
            pltpu.VMEM((heads, anchors, 2 * HEAD_DIM), BF16),
            pltpu.VMEM((heads, anchors, HEAD_DIM), BF16),
            pltpu.VMEM((heads, HEAD_DIM, anchors), BF16),
            pltpu.VMEM((anchors, TILE), F32),
            pltpu.VMEM((anchors, TILE), F32),
            pltpu.VMEM((anchors, TILE), F32),
            pltpu.VMEM((anchors, TILE), F32),
            pltpu.VMEM((anchors, TILE), BF16),
            pltpu.VMEM((anchors, TILE), BF16),
            pltpu.VMEM((heads, HEAD_DIM, anchors), F32),
            pltpu.VMEM((heads, HEAD_DIM, anchors), F32),
        ],
        compiler_params=pltpu.CompilerParams(vmem_limit_bytes=40 << 20),
        name="attention_grad",
    )(y, links, queries, out_grad, mine, other)


def link_table(link_cell, link_super, link_count, core):
    owners, slots = link_cell.shape
    live = jnp.arange(slots, dtype=jnp.int32)[None, :] < link_count[:, None]
    table = jnp.stack([jnp.where(live, link_cell, -1), jnp.where(live, link_super, -1)], axis=0)
    table = table.reshape(2, owners // N_CORE // GROUP, GROUP, N_CORE, slots)
    table = jnp.where(core == 0, table, table[:, :, :, ::-1])
    table = jnp.transpose(table, (1, 0, 3, 2, 4))
    place = (jnp.arange(N_CORE)[:, None] * GROUP + jnp.arange(GROUP)[None, :])[:, :, None] * 16
    place = place.astype(jnp.int32)
    cell, sup = table[:, 0], table[:, 1]
    low = jnp.where((sup >= 0) & (sup < 16), place + sup, -1)
    high = jnp.where(sup >= 16, place + sup - 16, -1)
    return jnp.stack([cell, low, high], axis=1).reshape(-1, 3, N_CORE * GROUP * slots)


def copies_kernel(keys_hbm, values_hbm, out_ref, keys_ref, values_ref, sems):
    loads = (
        pltpu.make_async_copy(keys_hbm, keys_ref, sems.at[0]),
        pltpu.make_async_copy(values_hbm, values_ref, sems.at[1]),
    )
    for load in loads:
        load.start()
    for load in loads:
        load.wait()
    pair = jnp.concatenate([keys_ref[...], values_ref[...]], axis=1)
    out_ref[...] = jnp.broadcast_to(pair[None], out_ref.shape)


def copies(keys, values):
    hbm = pl.BlockSpec(memory_space=pltpu.HBM)
    return pl.pallas_call(
        copies_kernel,
        in_specs=[hbm] * 2,
        out_specs=pl.BlockSpec(memory_space=pltpu.VMEM),
        out_shape=jax.ShapeDtypeStruct((N_Z, keys.shape[0], 2 * keys.shape[1]), BF16),
        scratch_shapes=[
            pltpu.VMEM(keys.shape, BF16),
            pltpu.VMEM(values.shape, BF16),
            pltpu.SemaphoreType.DMA((2,)),
        ],
        name="copies",
    )(keys, values)


def final_kernel(part_ref, key_ref, value_ref, super_ref):
    total = jnp.sum(part_ref[...].astype(F32), axis=0)
    anchors = key_ref.shape[0]
    cols = key_ref.shape[1]
    top = total[:anchors]
    for h in range(cols // HEAD_DIM):
        lanes = slice(h * HEAD_DIM, (h + 1) * HEAD_DIM)
        key_ref[:, lanes] = top[:, 2 * h * HEAD_DIM : (2 * h + 1) * HEAD_DIM]
        value_ref[:, lanes] = top[:, (2 * h + 1) * HEAD_DIM : (2 * h + 2) * HEAD_DIM]
    super_ref[0:16, :] = total[anchors:, :cols]
    super_ref[16:32, :] = total[anchors:, cols:]


def final(part, anchors, cols):
    vmem = pl.BlockSpec(memory_space=pltpu.VMEM)
    return pl.pallas_call(
        final_kernel,
        in_specs=[vmem],
        out_specs=[vmem] * 3,
        out_shape=[
            jax.ShapeDtypeStruct((anchors, cols), F32),
            jax.ShapeDtypeStruct((anchors, cols), F32),
            jax.ShapeDtypeStruct((SUP_DEV, cols), F32),
        ],
        compiler_params=pltpu.CompilerParams(vmem_limit_bytes=8 << 20),
        name="final",
    )(part)


def local(queries, anchor_keys, anchor_values, out_grad, link_cell, link_super, link_count):
    cols = queries.shape[0]
    partner = [(i, i ^ 1) for i in range(N_PB)]
    core = lax.axis_index("pb") % N_CORE
    spread = copies(anchor_keys, anchor_values)
    row = lax.all_to_all(spread, "pb", 0, 0, axis_index_groups=pb_groups("z"), tiled=True)
    row, link_cell, link_super, link_count = lax.optimization_barrier(
        (row, link_cell, link_super, link_count)
    )
    links = link_table(link_cell[0], link_super[0], link_count[0], core)
    rows = {d: lax.ppermute(row, "pb", y_shift(-d)) for d in (1, 3, 2)}
    mine = jnp.stack([row, rows[1], rows[2], rows[3]]).reshape(-1, 2 * cols)
    other = lax.ppermute(mine, "pb", partner)
    y = (lax.axis_index("pb") // (N_Z * N_CORE)).astype(jnp.int32).reshape(1)
    query_grad, keep, send = attention(y, links, queries, out_grad, mine, other)

    got = lax.ppermute(send, "pb", partner)
    part = (keep.astype(F32) + got.astype(F32)).astype(BF16).reshape(N_Y, N_Z, 32, 2 * cols)
    parts = [part[0]] + [lax.ppermute(part[d], "pb", y_shift(d)) for d in (2, 1, 3)]
    part = sum(p.astype(F32) for p in parts).astype(BF16)
    part = lax.all_to_all(part, "pb", 0, 0, axis_index_groups=pb_groups("z"), tiled=True)
    key_grad, value_grad, super_grad = final(part, anchor_keys.shape[0], cols)
    return (query_grad, key_grad, value_grad, super_grad)


def solution(mesh):
    return jax.shard_map(
        local,
        mesh=mesh,
        in_specs=(
            P("sa", "pb"),
            P("pb", "sa"),
            P("pb", "sa"),
            P("sa", "pb"),
            P("pb", None, None),
            P("pb", None, None),
            P("pb", None),
        ),
        out_specs=(P("sa", "pb"), P("pb", "sa"), P("pb", "sa"), P("pb", "sa")),
        check_vma=False,
    )
```
